32 devices in a mesh: shot: 2 (over x), tile: 16 (over z, y, core).
Axes of the slice: x: 2, y: 2, z: 4, core: 2. Of those that a mesh axis runs over, the one named last changes fastest.
Arguments:
- source: bfloat16 [16, 512, 4, 384], P('shot', 'tile'), parts along dimension 0, may hold values from -6 to 6
- receiver: bfloat16 [16, 512, 4, 384], P('shot', 'tile'), parts along dimension 0, may hold values from -6 to 6
- offsets: int32 [64], replicated, may hold values from -32 to 32, as said below
- snap_index: int32 [4], replicated, may hold values from 0 to 7, as said below
Outputs:
- image_lags: float32 [128, 512, 4, 384], P('shot', 'tile'), parts along dimension 0
The draws below stay inside these ranges and needn't reach their ends.
There are 2 independent parts, one for each index of `shot`. The reference program is written for one: setup_inputs(seed, part) draws one part's arguments, and reference() takes and returns one part's arrays. A program takes and returns all parts, laid end to end along the dimension named above; an argument that names none is the same for every part. Nothing has to cross between parts.
Inputs may be any that keep to these rules, and one draw needn't show every extreme that they name: `offsets`: distinct values; the lags -32 and 32 are always present. `snap_index`: distinct values; snapshots 0 and 7 are always present.
All inputs are finite; a program needn't handle non-finite values.
Results may differ from the reference program's by a relative error of at most 0.0003.
Values may be sent and summed in bfloat16 or wider, within the bound.
No kernel may reach another device: no remote copies, remote signals or barrier semaphores. Data moves between devices by JAX's collectives and lax.ppermute only.
A program may use at most 192 MiB of HBM per device.

```python
import jax
import jax.numpy as jnp
from jax import lax

CY = 4
NZ = 384
NLAG = 64
HMAX = 32
NSTORE = 8
NUSE = 4
NX = 512


def draw_offsets(key, part):
    key_one, key_two = jax.random.split(jax.random.fold_in(key, 11))
    interior = jax.random.permutation(key_one, 2 * HMAX - 1)[:NLAG - 2] - (HMAX - 1)
    complete = jnp.concatenate([interior.astype(jnp.int32), jnp.array([-HMAX, HMAX], jnp.int32)])
    return jax.random.permutation(key_two, complete).astype(jnp.int32)


def draw_snap_index(key, part):
    key_one, key_two = jax.random.split(jax.random.fold_in(key, 23))
    interior = jax.random.permutation(key_one, NSTORE - 2)[:NUSE - 2] + 1
    complete = jnp.concatenate([interior.astype(jnp.int32), jnp.array([0, NSTORE - 1], jnp.int32)])
    return jax.random.permutation(key_two, complete).astype(jnp.int32)


def levels(rng, shape, cuts, low, high):
    def one(position, shards_of):
        steps = jax.random.uniform(jax.random.fold_in(jax.random.fold_in(rng, 6), position), (shards_of,), jnp.float32, low / len(cuts), high / len(cuts))
        return jnp.repeat(jnp.exp(steps), shape[position] // shards_of).reshape((-1,) + (1,) * (len(shape) - position - 1))

    gain = one(*cuts[0])
    for cut in cuts[1:]:
        gain = gain * one(*cut)
    return gain


def noise(key, extent, scale, reach, pieces=(), dtype=jnp.bfloat16):
    values = jax.random.normal(key, extent, jnp.float32) * scale
    if len(pieces) > 0:
        values = levels(key, extent, pieces, -0.22, 0.18) * values
    return jnp.clip(values, min=-reach, max=reach).astype(dtype)


def setup_inputs(seed: int = 0, part: int = 0) -> dict:
    splits = jax.random.split(jax.random.key(seed), 5)
    own_keys = jax.random.split(jax.random.fold_in(splits[4], part), 5)
    return {
        "source": noise(own_keys[0], (NSTORE, NX, CY, NZ), 1.0, 6.0, ((1, 16),)),
        "receiver": noise(own_keys[1], (NSTORE, NX, CY, NZ), 1.0, 6.0, ((1, 16),)),
        "offsets": draw_offsets(jax.random.fold_in(splits[4], 71), part),
        "snap_index": draw_snap_index(jax.random.fold_in(splits[4], 71), part),
    }


def reference(source, receiver, offsets, snap_index):
    source_sel = jnp.take(source, snap_index, axis=0)
    receiver_sel = jnp.take(receiver, snap_index, axis=0)
    padding = ((0, 0), (HMAX, HMAX), (0, 0), (0, 0))
    source_sel = jnp.pad(source_sel, padding)
    receiver_sel = jnp.pad(receiver_sel, padding)
    weights = (jnp.arange(NUSE).astype(jnp.float32) + 1.0) / NUSE

    def per_offset(offset):
        left_start = (HMAX - offset).astype(jnp.int32)
        right_start = (HMAX + offset).astype(jnp.int32)
        shifted_src = lax.dynamic_slice_in_dim(source_sel, left_start, NX, 1)
        shifted_rec = lax.dynamic_slice_in_dim(receiver_sel, right_start, NX, 1)
        product = shifted_src.astype(jnp.float32) * shifted_rec.astype(jnp.float32)
        return jnp.sum(product * weights[:, None, None, None], axis=0)

    return lax.map(per_offset, offsets)
```

```python
import functools

import jax
import jax.numpy as jnp
from jax import lax
from jax.experimental import pallas as pl
from jax.experimental.pallas import tpu as pltpu
from jax.sharding import PartitionSpec as P

LANES = 128
BLOCK = 8
FAR = 8

ANY = pl.BlockSpec(memory_space=pl.ANY)
SMEM = pl.BlockSpec(memory_space=pltpu.SMEM)


def select_kernel(snap, source, receiver, whole, near, far, held, in_sem, out_sem):
    used, cells = held.shape[1], held.shape[2]
    reach = near.shape[3]
    odd = lax.axis_index("tile") % 2
    reads = []
    for field, stored in enumerate((source, receiver)):
        for j in range(used):
            copy = pltpu.make_async_copy(stored.at[snap[j]], held.at[field, j], in_sem.at[field, j])
            copy.start()
            reads.append(copy)
    for copy in reads:
        copy.wait()
    near_at = odd * (cells - reach)
    far_at = (1 - odd) * reach
    writes = []
    for k, (out, start) in enumerate(((near, near_at), (whole, 0), (far, far_at))):
        for z in range(out.shape[0]):
            copy = pltpu.make_async_copy(
                held.at[:, :, pl.ds(start, out.shape[3]), :, pl.ds(z * LANES, LANES)],
                out.at[z],
                out_sem.at[k, z],
            )
            copy.start()
            writes.append(copy)
    for copy in writes:
        copy.wait()


def select(source, receiver, snap_index, reach):
    _, cells, ny, nz = source.shape
    used, tiles = snap_index.shape[0], nz // LANES
    shape = lambda n: jax.ShapeDtypeStruct((tiles, 2, used, n, ny, LANES), source.dtype)
    return pl.pallas_call(
        select_kernel,
        out_shape=(shape(cells), shape(reach), shape(cells - reach)),
        in_specs=[SMEM, ANY, ANY],
        out_specs=(ANY, ANY, ANY),
        scratch_shapes=[
            pltpu.VMEM((2, used, cells, ny, nz), source.dtype),
            pltpu.SemaphoreType.DMA((2, used)),
            pltpu.SemaphoreType.DMA((3, tiles)),
        ],
        compiler_params=pltpu.CompilerParams(vmem_limit_bytes=8 << 20),
        name="select",
    )(snap_index, source, receiver)


def image_kernel(stage, places, ny, reach, *refs):
    count = len(places)
    offsets, pieces = refs[0], refs[1 : 1 + count]
    out, raw, wide, made, in_sem, out_sem = refs[-6:]
    tiles, used = wide.shape[0], wide.shape[2]
    cells = out.shape[1]
    odd = lax.axis_index("tile") % 2
    reads, at, base = [], [], 0
    for k, (piece, place) in enumerate(zip(pieces, places)):
        rows = piece.shape[3]
        copy = pltpu.make_async_copy(piece, raw.at[:, :, :, pl.ds(base, rows), :], in_sem.at[k])
        copy.start()
        reads.append(copy)
        n = rows // ny
        at.append({
            "centre": cells,
            "same": (1 - odd) * 2 * cells,
            "near": odd * 2 * cells + (1 - odd) * (cells - n),
            "far": odd * (3 * cells - n),
        }[place])
        base += rows
    base = 0
    for piece, copy, start in zip(pieces, reads, at):
        copy.wait()
        rows = piece.shape[3]
        for z in range(tiles):
            for j in range(used):
                weight = (j + 1.0) / used

                def widen(i, carry, z=z, j=j, base=base, start=start, weight=weight):
                    take = pl.ds(pl.multiple_of(base + i * 16, 16), 16)
                    put = pl.ds(pl.multiple_of(start * ny + i * 16, 16), 16)
                    wide[z, 0, j, put, :] = raw[z, 0, j, take, :].astype(jnp.float32) * weight
                    wide[z, 1, j, put, :] = raw[z, 1, j, take, :].astype(jnp.float32)
                    return carry

                lax.fori_loop(0, rows // 16, widen, 0, unroll=True)
        base += rows

    flat = made.reshape(made.shape[0], tiles, cells * ny, LANES)
    bands = {"local": (-cells, cells), "near": (cells, cells + reach), "far": (cells + reach, 2 * cells)}
    low, high = bands[stage]

    def one_lag(lag, written):
        h = offsets[lag]
        g = jnp.abs(h)
        first = jnp.clip(low - g, 0, cells)
        last = jnp.clip(high - g, 0, cells)
        lo = jnp.where(odd == 1, first, cells - last)
        hi = jnp.where(odd == 1, last, cells - first)
        some = last > first
        block_lo = jnp.where(some, lo // BLOCK, 0)
        block_hi = jnp.where(some, (hi + BLOCK - 1) // BLOCK, 0)

        def one_block(block, carry):
            x = block * BLOCK
            left = (x - h + cells) * ny
            right = (x + h + cells) * ny
            for z in range(tiles):
                for i in range(BLOCK * ny // 8):
                    total = None
                    for j in range(used):
                        term = wide[z, 0, j, pl.ds(left + 8 * i, 8), :] * wide[z, 1, j, pl.ds(right + 8 * i, 8), :]
                        total = term if total is None else total + term
                    flat[lag, z, pl.ds(pl.multiple_of(x * ny, 8) + 8 * i, 8), :] = total
                pltpu.make_async_copy(
                    made.at[lag, z, pl.ds(x, BLOCK)],
                    out.at[lag, pl.ds(x, BLOCK), :, pl.ds(z * LANES, LANES)],
                    out_sem,
                ).start()
            return carry

        lax.fori_loop(block_lo, block_hi, one_block, 0)
        return written + block_hi - block_lo

    written = lax.fori_loop(0, offsets.shape[0], one_lag, 0)
    per_lag = cells // BLOCK
    whole_lags = written // per_lag
    size = 1
    while size < made.shape[0] * 2:
        span = min(size, made.shape[0])

        @pl.when((whole_lags & size) != 0)
        def _(span=span):
            done = made.at[pl.ds(0, span)]
            pltpu.make_async_copy(done, done, out_sem).wait()

        size *= 2

    def rest(i, carry):
        done = made.at[0, :, pl.ds(0, BLOCK)]
        pltpu.make_async_copy(done, done, out_sem).wait()
        return carry

    lax.fori_loop(0, written - whole_lags * per_lag, rest, 0)


def image(stage, offsets, pieces, image_so_far, shape, reach):
    lags, cells, ny, nz = shape
    tiles = nz // LANES
    places, arrays = zip(*pieces)
    used = arrays[0].shape[2]
    arrays = [a.reshape(tiles, 2, used, -1, LANES) for a in arrays]
    rows = sum(a.shape[3] for a in arrays)
    operands = [offsets, *arrays]
    specs = [SMEM] + [ANY] * len(arrays)
    aliases = {}
    if image_so_far is not None:
        aliases = {len(operands): 0}
        operands.append(image_so_far)
        specs.append(ANY)
    share = {"local": 0.5, "near": 0.46, "far": 0.04}[stage]
    work = lags * cells * ny * nz
    return pl.pallas_call(
        functools.partial(image_kernel, stage, places, ny, reach),
        out_shape=jax.ShapeDtypeStruct(shape, jnp.float32),
        in_specs=specs,
        out_specs=ANY,
        scratch_shapes=[
            pltpu.VMEM((tiles, 2, used, rows, LANES), arrays[0].dtype),
            pltpu.VMEM((tiles, 2, used, 3 * cells * ny, LANES), jnp.float32),
            pltpu.VMEM((lags, tiles, cells, ny, LANES), jnp.float32),
            pltpu.SemaphoreType.DMA((len(arrays),)),
            pltpu.SemaphoreType.DMA,
        ],
        input_output_aliases=aliases,
        compiler_params=pltpu.CompilerParams(vmem_limit_bytes=28 << 20),
        cost_estimate=pl.CostEstimate(
            flops=int(8 * share * work), bytes_accessed=int(4 * share * work), transcendentals=0
        ),
        name=stage,
    )(*operands)


def local(source, receiver, offsets, snap_index):
    _, cells, ny, nz = source.shape
    shape = (offsets.shape[0], cells, ny, nz)
    reach = cells - FAR
    devices = lax.axis_size("tile")
    same = [(i, i ^ 1) for i in range(devices) if i ^ 1 < devices]
    cross = [(i, ((i + 1) ^ 1) - 1) for i in range(1, devices)]
    cross = [(i, j) for i, j in cross if j < devices]
    whole, near, far = select(source, receiver, snap_index, reach)
    with jax.named_scope("cross_near"):
        got_near = lax.ppermute(near, "tile", cross)
    with jax.named_scope("in_chip"):
        got_same = lax.ppermute(whole, "tile", same)
    with jax.named_scope("cross_far"):
        got_far = lax.ppermute(far, "tile", cross)
    pieces = [("centre", whole), ("same", got_same)]
    made = image("local", offsets, pieces, None, shape, reach)
    pieces.append(("near", got_near))
    made = image("near", offsets, pieces, made, shape, reach)
    pieces.append(("far", got_far))
    return image("far", offsets, pieces, made, shape, reach)


def solution(mesh):
    return jax.shard_map(
        local,
        mesh=mesh,
        in_specs=(P("shot", "tile", None, None), P("shot", "tile", None, None), P(), P()),
        out_specs=P("shot", "tile", None, None),
        check_vma=False,
    )
```

```python
import functools

import jax
import jax.numpy as jnp
from jax import lax
from jax.experimental import pallas as pl
from jax.experimental.pallas import tpu as pltpu
from jax.sharding import PartitionSpec as P

HMAX = 32
LANES = 128
SUB = 8
BLOCK = 8
FAR = 8
GROUP = 4

ANY = pl.BlockSpec(memory_space=pl.ANY)
SMEM = pl.BlockSpec(memory_space=pltpu.SMEM)
VMEM = pl.BlockSpec(memory_space=pltpu.VMEM)


def in_vmem(x):
    return pltpu.with_memory_space_constraint(x, pltpu.VMEM)


def in_smem(x):
    return pltpu.with_memory_space_constraint(x, pltpu.SMEM)


def in_hbm(x):
    return pltpu.with_memory_space_constraint(x, pltpu.HBM)


def select_kernel(edge, snap_hbm, source, receiver, out, snap, snap_sem, sem):
    tiles, _, used, take = out.shape[:4]
    cells = source.shape[1]
    load = pltpu.make_async_copy(snap_hbm, snap, snap_sem)
    load.start()
    start = (lax.axis_index("tile") % 2) * (cells - take) if edge else 0
    load.wait()
    copies = []
    for field, stored in enumerate((source, receiver)):
        for j in range(used):
            for z in range(tiles):
                copy = pltpu.make_async_copy(
                    stored.at[snap[j], pl.ds(start, take), :, pl.ds(z * LANES, LANES)],
                    out.at[z, field, j],
                    sem.at[field, j, z],
                )
                copy.start()
                copies.append(copy)
    for copy in copies:
        copy.wait()


def select(source, receiver, snap_index, take, edge):
    _, _, ny, nz = source.shape
    used, tiles = snap_index.shape[0], nz // LANES
    return pl.pallas_call(
        functools.partial(select_kernel, edge),
        out_shape=pltpu.VMEM((tiles, 2, used, take, ny, LANES), source.dtype),
        in_specs=[ANY, ANY, ANY],
        out_specs=VMEM,
        scratch_shapes=[
            pltpu.SMEM(snap_index.shape, snap_index.dtype),
            pltpu.SemaphoreType.DMA,
            pltpu.SemaphoreType.DMA((2, used, tiles)),
        ],
        compiler_params=pltpu.CompilerParams(vmem_limit_bytes=8 << 20),
    )(in_hbm(snap_index), in_hbm(source), in_hbm(receiver))


def widen(piece, wide, start, ny):
    tiles, _, used, rows = piece.shape[:4]
    for z in range(tiles):
        for j in range(used):
            for field, weight in ((0, (j + 1.0) / used), (1, 1.0)):

                def some(i, carry, z=z, j=j, field=field, weight=weight):
                    take = pl.ds(pl.multiple_of(i * 32, 32), 32)
                    put = pl.ds(pl.multiple_of(start * ny + i * 32, 32), 32)
                    value = piece[z, field, j, take, :].astype(jnp.float32)
                    wide[z, field, j, put, :] = value if weight == 1.0 else value * weight
                    return carry

                lax.fori_loop(0, rows // 32, some, 0, unroll=True)


def local_kernel(offsets_hbm, whole, same, out, wide, far, slots, offsets, made, load_sem, far_sem, out_sem):
    load = pltpu.make_async_copy(offsets_hbm, offsets, load_sem)
    load.start()
    tiles, _, used = wide.shape[:3]
    cells, ny = out.shape[1:3]
    odd = lax.axis_index("tile") % 2
    reach = cells - far.shape[3]
    copy_far = pltpu.make_async_copy(
        whole.at[:, :, :, pl.ds((1 - odd) * reach, far.shape[3])], far, far_sem
    )
    copy_far.start()
    flat_shape = (tiles, 2, used, cells * ny, LANES)
    widen(whole.reshape(flat_shape), wide, cells, ny)
    widen(same, wide, (1 - odd) * 2 * cells, ny)
    load.wait()
    for h in range(2 * HMAX + 1):
        slots[h] = -1
    for lag in range(offsets.shape[0]):
        slots[offsets[lag] + HMAX] = lag
    flat = made.reshape(made.shape[0], tiles, cells * ny, LANES)

    def one_lag(lag, written):
        h = offsets[lag]
        count = cells - jnp.abs(h)
        blocks = (count + BLOCK - 1) // BLOCK
        first = jnp.where(odd == 1, 0, cells // BLOCK - blocks)

        def one_block(block, carry):
            x = block * BLOCK
            left = (x - h + cells) * ny
            right = (x + h + cells) * ny
            for z in range(tiles):
                for i in range(BLOCK * ny // SUB):
                    total = None
                    for j in range(used):
                        term = (
                            wide[z, 0, j, pl.ds(left + SUB * i, SUB), :]
                            * wide[z, 1, j, pl.ds(right + SUB * i, SUB), :]
                        )
                        total = term if total is None else total + term
                    flat[lag, z, pl.ds(pl.multiple_of(x * ny, SUB) + SUB * i, SUB), :] = total
                pltpu.make_async_copy(
                    made.at[lag, z, pl.ds(x, BLOCK)],
                    out.at[lag, pl.ds(x, BLOCK), :, pl.ds(z * LANES, LANES)],
                    out_sem,
                ).start()
            return carry

        lax.fori_loop(first, first + blocks, one_block, 0)
        return written + blocks

    written = lax.fori_loop(0, offsets.shape[0], one_lag, 0)
    per_lag = cells // BLOCK
    whole_lags = written // per_lag
    size = 1
    while size <= made.shape[0]:

        @pl.when((whole_lags & size) != 0)
        def _(span=size):
            done = made.at[pl.ds(0, span)]
            pltpu.make_async_copy(done, done, out_sem).wait()

        size *= 2

    def rest(i, carry):
        done = made.at[0, :, pl.ds(0, BLOCK)]
        pltpu.make_async_copy(done, done, out_sem).wait()
        return carry

    lax.fori_loop(0, written - whole_lags * per_lag, rest, 0)
    copy_far.wait()


def band_kernel(skip, slots, piece, wide_in, image_in, out, wide, made, sem):
    del wide_in, image_in
    tiles, _, used, rows = piece.shape[:4]
    cells, ny = out.shape[1:3]
    width = rows // ny
    odd = lax.axis_index("tile") % 2
    is_odd = odd == 1
    begin = jnp.where(is_odd, 2 * cells + skip, cells - skip - width)
    widen(piece, wide, begin, ny)
    flat = made.reshape(2, HMAX, tiles, width * ny, LANES)
    copies = []
    for sign in range(2):
        field = jnp.where(is_odd, 1 - sign, sign)
        for low in range(skip, HMAX, GROUP):
            longest = min(low + GROUP - skip, width)
            for m in range((longest + BLOCK - 1) // BLOCK):
                row = jnp.where(is_odd, BLOCK * m, width - BLOCK * (m + 1))
                anchor = begin + row
                shift = 2 * (low + 1)
                other = anchor + jnp.where(is_odd, -shift - 2 * (GROUP - 1), shift)
                per = BLOCK * ny // SUB
                for z in range(tiles):
                    totals = [[None] * per for _ in range(GROUP)]
                    for j in range(used):
                        a = [
                            wide[z, field, j, pl.ds(pl.multiple_of(anchor * ny, SUB) + SUB * i, SUB), :]
                            for i in range(per)
                        ]
                        b = [
                            wide[z, 1 - field, j, pl.ds(pl.multiple_of(other * ny, SUB) + SUB * i, SUB), :]
                            for i in range(per + GROUP - 1)
                        ]
                        for t in range(GROUP):
                            for i in range(per):
                                term = a[i] * b[i + t]
                                totals[t][i] = term if j == 0 else totals[t][i] + term
                    for t in range(GROUP):
                        lag_at = low + jnp.where(is_odd, GROUP - 1 - t, t)
                        for i in range(per):
                            flat[sign, lag_at, z, pl.ds(pl.multiple_of(row * ny, SUB) + SUB * i, SUB), :] = totals[t][i]
            for g in range(low + 1, low + GROUP + 1):
                length = min(g - skip, width)
                slot = slots[HMAX + (g if sign == 0 else -g)]
                x = jnp.where(is_odd, cells + skip - g, g - skip - length)
                row = jnp.where(is_odd, 0, width - length)
                ends = []
                for z in range(tiles):
                    ends.append((
                        made.at[sign, g - 1, z, pl.ds(row, length)],
                        out.at[jnp.maximum(slot, 0), pl.ds(x, length), :, pl.ds(z * LANES, LANES)],
                    ))

                @pl.when(slot >= 0)
                def _(ends=ends):
                    for here, there in ends:
                        pltpu.make_async_copy(here, there, sem).start()

                copies.append((slot, ends))
    for slot, ends in copies:

        @pl.when(slot >= 0)
        def _(ends=ends):
            for here, there in ends:
                pltpu.make_async_copy(here, there, sem).wait()


def band(skip, slots, piece, wide, image, share):
    tiles, _, used, n, ny, _ = piece.shape
    return pl.pallas_call(
        functools.partial(band_kernel, skip),
        out_shape=(
            jax.ShapeDtypeStruct(image.shape, image.dtype),
            pltpu.VMEM(wide.shape, wide.dtype),
        ),
        in_specs=[SMEM, VMEM, VMEM, ANY],
        out_specs=(ANY, VMEM),
        scratch_shapes=[
            pltpu.VMEM((2, HMAX, tiles, n, ny, LANES), jnp.float32),
            pltpu.SemaphoreType.DMA,
        ],
        input_output_aliases={2: 1, 3: 0},
        compiler_params=pltpu.CompilerParams(vmem_limit_bytes=20 << 20),
        cost_estimate=pl.CostEstimate(
            flops=int(8 * share * image.size), bytes_accessed=int(4 * share * image.size), transcendentals=0
        ),
    )(in_smem(slots), in_vmem(piece.reshape(tiles, 2, used, n * ny, LANES)), in_vmem(wide), image)


def local_part(offsets, whole, same, shape, far):
    tiles, _, used, cells, ny, _ = whole.shape
    lags = shape[0]
    size = shape[0] * shape[1] * shape[2] * shape[3]
    return pl.pallas_call(
        local_kernel,
        out_shape=(
            jax.ShapeDtypeStruct(shape, jnp.float32),
            pltpu.VMEM((tiles, 2, used, 3 * cells * ny, LANES), jnp.float32),
            pltpu.VMEM((tiles, 2, used, far, ny, LANES), whole.dtype),
            pltpu.SMEM((2 * HMAX + 1,), offsets.dtype),
        ),
        in_specs=[ANY, VMEM, VMEM],
        out_specs=(ANY, VMEM, VMEM, SMEM),
        scratch_shapes=[
            pltpu.SMEM(offsets.shape, offsets.dtype),
            pltpu.VMEM((lags, tiles, cells, ny, LANES), jnp.float32),
            pltpu.SemaphoreType.DMA,
            pltpu.SemaphoreType.DMA,
            pltpu.SemaphoreType.DMA,
        ],
        compiler_params=pltpu.CompilerParams(vmem_limit_bytes=20 << 20),
        cost_estimate=pl.CostEstimate(flops=4 * size, bytes_accessed=2 * size, transcendentals=0),
        name="local",
    )(in_hbm(offsets), in_vmem(whole), in_vmem(same.reshape(tiles, 2, used, cells * ny, LANES)))


def local(source, receiver, offsets, snap_index):
    _, cells, ny, nz = source.shape
    shape = (offsets.shape[0], cells, ny, nz)
    assert cells == HMAX
    devices = lax.axis_size("tile")
    same = [(i, i ^ 1) for i in range(devices) if i ^ 1 < devices]
    cross = [(i, ((i + 1) ^ 1) - 1) for i in range(1, devices)]
    cross = [(i, j) for i, j in cross if j < devices]
    near = select(source, receiver, snap_index, cells - FAR, True)
    got_near = lax.ppermute(near, "tile", cross)
    whole = select(source, receiver, snap_index, cells, False)
    got_same = lax.ppermute(whole, "tile", same)
    made, wide, far, slots = local_part(offsets, whole, got_same, shape, FAR)
    got_far = lax.ppermute(far, "tile", cross)
    made, wide = band(0, slots, got_near, wide, made, 0.46)
    return band(cells - FAR, slots, got_far, wide, made, 0.04)[0]


def solution(mesh):
    return jax.shard_map(
        local,
        mesh=mesh,
        in_specs=(P("shot", "tile", None, None), P("shot", "tile", None, None), P(), P()),
        out_specs=P("shot", "tile", None, None),
        check_vma=False,
    )
```

```python
import functools

import jax
import jax.numpy as jnp
from jax import lax
from jax.experimental import pallas as pl
from jax.experimental.pallas import tpu as pltpu
from jax.sharding import PartitionSpec as P

HMAX = 32
LANES = 128
SUB = 8
BLOCK = 4
FAR = 12
PAD = 8
GROUP = 4

ANY = pl.BlockSpec(memory_space=pl.ANY)
SMEM = pl.BlockSpec(memory_space=pltpu.SMEM)
VMEM = pl.BlockSpec(memory_space=pltpu.VMEM)


def in_vmem(x):
    return pltpu.with_memory_space_constraint(x, pltpu.VMEM)


def in_smem(x):
    return pltpu.with_memory_space_constraint(x, pltpu.SMEM)


def in_hbm(x):
    return pltpu.with_memory_space_constraint(x, pltpu.HBM)


def select_kernel(part, snap_hbm, source, receiver, out, snap, snap_sem, sem):
    tiles, _, used, take = out.shape[:4]
    cells = source.shape[1]
    load = pltpu.make_async_copy(snap_hbm, snap, snap_sem)
    load.start()
    odd = lax.axis_index("tile") % 2
    start = {"near": odd * (cells - take), "far": (1 - odd) * (cells - take), "whole": 0}[part]
    load.wait()
    copies = []
    for field, stored in enumerate((source, receiver)):
        for j in range(used):
            for z in range(tiles):
                copy = pltpu.make_async_copy(
                    stored.at[snap[j], pl.ds(start, take), :, pl.ds(z * LANES, LANES)],
                    out.at[z, field, j],
                    sem.at[field, j, z],
                )
                copy.start()
                copies.append(copy)
    for copy in copies:
        copy.wait()


def select(part, source, receiver, snap_index, take):
    _, _, ny, nz = source.shape
    used, tiles = snap_index.shape[0], nz // LANES
    return pl.pallas_call(
        functools.partial(select_kernel, part),
        out_shape=pltpu.VMEM((tiles, 2, used, take, ny, LANES), source.dtype),
        in_specs=[ANY, ANY, ANY],
        out_specs=VMEM,
        scratch_shapes=[
            pltpu.SMEM(snap_index.shape, snap_index.dtype),
            pltpu.SemaphoreType.DMA,
            pltpu.SemaphoreType.DMA((2, used, tiles)),
        ],
        compiler_params=pltpu.CompilerParams(vmem_limit_bytes=8 << 20),
    )(in_hbm(snap_index), in_hbm(source), in_hbm(receiver))


def widen(piece, wide, start, ny):
    tiles, _, used, rows = piece.shape[:4]
    for z in range(tiles):
        for j in range(used):
            for field, weight in ((0, (j + 1.0) / used), (1, 1.0)):

                def some(i, carry, z=z, j=j, field=field, weight=weight):
                    take = pl.ds(pl.multiple_of(i * 16, 16), 16)
                    put = pl.ds(pl.multiple_of(start * ny + i * 16, 16), 16)
                    value = piece[z, field, j, take, :].astype(jnp.float32)
                    wide[z, field, j, put, :] = value if weight == 1.0 else value * weight
                    return carry

                lax.fori_loop(0, rows // 16, some, 0, unroll=True)


def image_band(skip, width, slots, out, wide, made, sem):
    tiles, _, used = wide.shape[:3]
    cells, ny = out.shape[1:3]
    is_odd = lax.axis_index("tile") % 2 == 1
    begin = PAD + jnp.where(is_odd, 2 * cells + skip, cells - skip - width)
    flat = made.reshape(2, HMAX, tiles, width * ny, LANES)
    per = BLOCK * ny // SUB

    def extent(g):
        first = max(0, g - cells - skip)
        return first, max(0, min(g - skip, width) - first)

    def rows(cell, i):
        return pl.ds(pl.multiple_of(cell * ny, SUB) + SUB * i, SUB)

    copies = []
    for sign in range(2):
        field = jnp.where(is_odd, 1 - sign, sign)
        for low in range(max(skip, 0), HMAX, GROUP):
            spans = [extent(g) for g in range(low + 1, low + GROUP + 1)]
            spans = [(first, first + length) for first, length in spans if length > 0]
            from_block = min(first for first, _ in spans) // BLOCK
            to_block = -(-max(last for _, last in spans) // BLOCK)
            for m in range(from_block, to_block):
                row = jnp.where(is_odd, BLOCK * m, width - BLOCK * (m + 1))
                anchor = begin + row
                shift = 2 * (low + 1)
                other = anchor + jnp.where(is_odd, -shift - 2 * (GROUP - 1), shift)
                assert cells + skip + BLOCK * m + cells - shift - 2 * (GROUP - 1) >= -PAD
                for z in range(tiles):
                    totals = [[None] * per for _ in range(GROUP)]
                    for j in range(used):
                        a = [wide[z, field, j, rows(anchor, i), :] for i in range(per)]
                        b = [wide[z, 1 - field, j, rows(other, i), :] for i in range(per + GROUP - 1)]
                        for t in range(GROUP):
                            for i in range(per):
                                term = a[i] * b[i + t]
                                totals[t][i] = term if j == 0 else totals[t][i] + term
                    for t in range(GROUP):
                        lag_at = low + jnp.where(is_odd, GROUP - 1 - t, t)
                        for i in range(per):
                            flat[sign, lag_at, z, rows(row, i), :] = totals[t][i]
            for g in range(low + 1, low + GROUP + 1):
                first, length = extent(g)
                if length == 0:
                    continue
                row = jnp.where(is_odd, first, width - first - length)
                x = row + jnp.where(is_odd, cells + skip - g, g - skip - width)
                slot = slots[HMAX + (g if sign == 0 else -g)]
                copies.append((slot, send(made.at[sign, g - 1], row, out, slot, x, length, sem)))
    return copies


def send(here, row, out, slot, x, length, sem):
    pairs = [
        (
            here.at[z, pl.ds(row, length)],
            out.at[jnp.maximum(slot, 0), pl.ds(x, length), :, pl.ds(z * LANES, LANES)],
        )
        for z in range(here.shape[0])
    ]

    @pl.when(slot >= 0)
    def _():
        for source, target in pairs:
            pltpu.make_async_copy(source, target, sem).start()

    return pairs


def finish(copies, sem):
    for slot, pairs in copies:

        @pl.when(slot >= 0)
        def _(pairs=pairs):
            for source, target in pairs:
                pltpu.make_async_copy(source, target, sem).wait()


def local_kernel(offsets_hbm, whole, same, out, wide, slots, offsets, made, zero, load_sem, out_sem):
    load = pltpu.make_async_copy(offsets_hbm, offsets, load_sem)
    load.start()
    tiles, _, used = wide.shape[:3]
    cells, ny = out.shape[1:3]
    odd = lax.axis_index("tile") % 2
    widen(whole.reshape(tiles, 2, used, cells * ny, LANES), wide, PAD + cells, ny)
    widen(same, wide, PAD + (1 - odd) * 2 * cells, ny)
    load.wait()
    for h in range(2 * HMAX + 1):
        slots[h] = -1
    for lag in range(offsets.shape[0]):
        slots[offsets[lag] + HMAX] = lag
    flat = zero.reshape(tiles, cells * ny, LANES)

    def no_lag(i, carry):
        here = pl.ds(pl.multiple_of(i * SUB, SUB), SUB)
        there = pl.ds((PAD + cells) * ny + pl.multiple_of(i * SUB, SUB), SUB)
        for z in range(tiles):
            total = None
            for j in range(used):
                term = wide[z, 0, j, there, :] * wide[z, 1, j, there, :]
                total = term if total is None else total + term
            flat[z, here, :] = total
        return carry

    lax.fori_loop(0, cells * ny // SUB, no_lag, 0)
    copies = [(slots[HMAX], send(zero, 0, out, slots[HMAX], 0, cells, out_sem))]
    copies += image_band(-cells, cells, slots, out, wide, made, out_sem)
    finish(copies, out_sem)


def band_kernel(skip, slots, piece, wide_in, image_in, out, wide, made, sem):
    del wide_in, image_in
    cells, ny = out.shape[1:3]
    width = piece.shape[3] // ny
    is_odd = lax.axis_index("tile") % 2 == 1
    widen(piece, wide, PAD + jnp.where(is_odd, 2 * cells + skip, cells - skip - width), ny)
    finish(image_band(skip, width, slots, out, wide, made, sem), sem)


def band(skip, slots, piece, wide, image, share):
    tiles, _, used, n, ny, _ = piece.shape
    return pl.pallas_call(
        functools.partial(band_kernel, skip),
        out_shape=(
            jax.ShapeDtypeStruct(image.shape, image.dtype),
            pltpu.VMEM(wide.shape, wide.dtype),
        ),
        in_specs=[SMEM, VMEM, VMEM, ANY],
        out_specs=(ANY, VMEM),
        scratch_shapes=[
            pltpu.VMEM((2, HMAX, tiles, n, ny, LANES), jnp.float32),
            pltpu.SemaphoreType.DMA,
        ],
        input_output_aliases={2: 1, 3: 0},
        compiler_params=pltpu.CompilerParams(vmem_limit_bytes=20 << 20),
        cost_estimate=pl.CostEstimate(
            flops=int(8 * share * image.size), bytes_accessed=int(4 * share * image.size), transcendentals=0
        ),
    )(in_smem(slots), in_vmem(piece.reshape(tiles, 2, used, n * ny, LANES)), in_vmem(wide), image)


def local_part(offsets, whole, same, shape):
    tiles, _, used, cells, ny, _ = whole.shape
    size = shape[0] * shape[1] * shape[2] * shape[3]
    return pl.pallas_call(
        local_kernel,
        out_shape=(
            jax.ShapeDtypeStruct(shape, jnp.float32),
            pltpu.VMEM((tiles, 2, used, (3 * cells + 2 * PAD) * ny, LANES), jnp.float32),
            pltpu.SMEM((2 * HMAX + 1,), offsets.dtype),
        ),
        in_specs=[ANY, VMEM, VMEM],
        out_specs=(ANY, VMEM, SMEM),
        scratch_shapes=[
            pltpu.SMEM(offsets.shape, offsets.dtype),
            pltpu.VMEM((2, HMAX, tiles, cells, ny, LANES), jnp.float32),
            pltpu.VMEM((tiles, cells, ny, LANES), jnp.float32),
            pltpu.SemaphoreType.DMA,
            pltpu.SemaphoreType.DMA,
        ],
        compiler_params=pltpu.CompilerParams(vmem_limit_bytes=20 << 20),
        cost_estimate=pl.CostEstimate(flops=4 * size, bytes_accessed=2 * size, transcendentals=0),
        name="local",
    )(in_hbm(offsets), in_vmem(whole), in_vmem(same.reshape(tiles, 2, used, cells * ny, LANES)))


def local(source, receiver, offsets, snap_index):
    _, cells, ny, nz = source.shape
    shape = (offsets.shape[0], cells, ny, nz)
    assert cells == HMAX
    devices = lax.axis_size("tile")
    same = [(i, i ^ 1) for i in range(devices) if i ^ 1 < devices]
    cross = [(i, ((i + 1) ^ 1) - 1) for i in range(1, devices)]
    cross = [(i, j) for i, j in cross if j < devices]
    take = functools.partial(select, source=source, receiver=receiver, snap_index=snap_index)
    near = take("near", take=cells - FAR)
    got_near = lax.ppermute(near, "tile", cross)
    whole = take("whole", take=cells)
    got_same = lax.ppermute(whole, "tile", same)
    far = take("far", take=FAR)
    got_far = lax.ppermute(far, "tile", cross)
    made, wide, slots = local_part(offsets, whole, got_same, shape)
    made, wide = band(0, slots, got_near, wide, made, 0.46)
    return band(cells - FAR, slots, got_far, wide, made, 0.04)[0]


def solution(mesh):
    return jax.shard_map(
        local,
        mesh=mesh,
        in_specs=(P("shot", "tile", None, None), P("shot", "tile", None, None), P(), P()),
        out_specs=P("shot", "tile", None, None),
        check_vma=False,
    )
```

```python
import functools

import jax
import jax.numpy as jnp
from jax import lax
from jax.experimental import pallas as pl
from jax.experimental.pallas import tpu as pltpu
from jax.sharding import PartitionSpec as P

HMAX = 32
LANES = 128
SUB = 8
BLOCK = 4
FAR = 12
ENDS = 2
PAD = 8
GROUP = 4

ANY = pl.BlockSpec(memory_space=pl.ANY)
SMEM = pl.BlockSpec(memory_space=pltpu.SMEM)
VMEM = pl.BlockSpec(memory_space=pltpu.VMEM)


def in_vmem(x):
    return pltpu.with_memory_space_constraint(x, pltpu.VMEM)


def in_smem(x):
    return pltpu.with_memory_space_constraint(x, pltpu.SMEM)


def in_hbm(x):
    return pltpu.with_memory_space_constraint(x, pltpu.HBM)


def gather(source, receiver, chosen, start, out, sem):
    copies = []
    for field, stored in enumerate((source, receiver)):
        for k, snapshot in enumerate(chosen):
            for z in range(out.shape[0]):
                copy = pltpu.make_async_copy(
                    stored.at[snapshot, pl.ds(start, out.shape[3]), :, pl.ds(z * LANES, LANES)],
                    out.at[z, field, k],
                    sem.at[field, k, z],
                )
                copy.start()
                copies.append(copy)
    return copies


def near_start(cells, take):
    return (lax.axis_index("tile") % 2) * (cells - take)


def select_ends_kernel(snap_hbm, source, receiver, out, order, weights, snap, snap_sem, sem):
    load = pltpu.make_async_copy(snap_hbm, snap, snap_sem)
    load.start()
    final = source.shape[0] - 1
    start = near_start(source.shape[1], out.shape[3])
    copies = gather(source, receiver, (0, final), start, out, sem)
    load.wait()
    used = snap.shape[0]
    other = jnp.int32(ENDS)
    for j in range(used):
        snapshot = snap[j]
        is_end = (snapshot == 0) | (snapshot == final)
        at = jnp.where(is_end, jnp.where(snapshot == 0, 0, 1), jnp.minimum(other, used - 1))
        order[at] = snapshot
        weights[at] = (j + 1.0) / used
        other = other + jnp.where(is_end, 0, 1)
    for copy in copies:
        copy.wait()


def select_kernel(part, order, source, receiver, out, sem):
    used, cells = order.shape[0], source.shape[1]
    count, take = out.shape[2:4]
    start = near_start(cells, take)
    start = {"others": start, "far": cells - take - start, "whole": 0}[part]
    chosen = [order[k] for k in range(used - count, used)]
    for copy in gather(source, receiver, chosen, start, out, sem):
        copy.wait()


def select_ends(source, receiver, snap_index, take):
    _, _, ny, nz = source.shape
    tiles = nz // LANES
    return pl.pallas_call(
        select_ends_kernel,
        out_shape=(
            pltpu.VMEM((tiles, 2, ENDS, take, ny, LANES), source.dtype),
            pltpu.SMEM(snap_index.shape, snap_index.dtype),
            pltpu.SMEM(snap_index.shape, jnp.float32),
        ),
        in_specs=[ANY, ANY, ANY],
        out_specs=(VMEM, SMEM, SMEM),
        scratch_shapes=[
            pltpu.SMEM(snap_index.shape, snap_index.dtype),
            pltpu.SemaphoreType.DMA,
            pltpu.SemaphoreType.DMA((2, ENDS, tiles)),
        ],
        compiler_params=pltpu.CompilerParams(vmem_limit_bytes=8 << 20),
        name="select_ends",
    )(in_hbm(snap_index), in_hbm(source), in_hbm(receiver))


def select(part, source, receiver, order, count, take):
    _, _, ny, nz = source.shape
    tiles = nz // LANES
    return pl.pallas_call(
        functools.partial(select_kernel, part),
        out_shape=pltpu.VMEM((tiles, 2, count, take, ny, LANES), source.dtype),
        in_specs=[SMEM, ANY, ANY],
        out_specs=VMEM,
        scratch_shapes=[pltpu.SemaphoreType.DMA((2, count, tiles))],
        compiler_params=pltpu.CompilerParams(vmem_limit_bytes=8 << 20),
    )(in_smem(order), in_hbm(source), in_hbm(receiver))


def widen(piece, wide, start, ny, weights, base=0):
    tiles, _, count, rows = piece.shape[:4]
    for k in range(count):
        weight = weights[base + k]
        for z in range(tiles):
            for i in range(0, rows, 16):
                take = pl.ds(i, 16)
                put = pl.ds(pl.multiple_of(start * ny, 16) + i, 16)
                wide[z, 0, base + k, put, :] = piece[z, 0, k, take, :].astype(jnp.float32) * weight
                wide[z, 1, base + k, put, :] = piece[z, 1, k, take, :].astype(jnp.float32)


def image_band(skip, width, slots, out, wide, made, sem):
    tiles, _, used = wide.shape[:3]
    cells, ny = out.shape[1:3]
    is_odd = lax.axis_index("tile") % 2 == 1
    begin = PAD + jnp.where(is_odd, 2 * cells + skip, cells - skip - width)
    flat = made.reshape(2, HMAX, tiles, width * ny, LANES)
    per = BLOCK * ny // SUB

    def extent(g):
        first = max(0, g - cells - skip)
        return first, max(0, min(g - skip, width) - first)

    def rows(cell, i):
        return pl.ds(pl.multiple_of(cell * ny, SUB) + SUB * i, SUB)

    copies = []
    for sign in range(2):
        field = jnp.where(is_odd, 1 - sign, sign)
        for low in range(max(skip, 0), HMAX, GROUP):
            spans = [extent(g) for g in range(low + 1, low + GROUP + 1)]
            spans = [(first, first + length) for first, length in spans if length > 0]
            from_block = min(first for first, _ in spans) // BLOCK
            to_block = -(-max(last for _, last in spans) // BLOCK)
            for m in range(from_block, to_block):
                row = jnp.where(is_odd, BLOCK * m, width - BLOCK * (m + 1))
                anchor = begin + row
                shift = 2 * (low + 1)
                other = anchor + jnp.where(is_odd, -shift - 2 * (GROUP - 1), shift)
                assert cells + skip + BLOCK * m + cells - shift - 2 * (GROUP - 1) >= -PAD
                for z in range(tiles):
                    totals = [[None] * per for _ in range(GROUP)]
                    for j in range(used):
                        a = [wide[z, field, j, rows(anchor, i), :] for i in range(per)]
                        b = [wide[z, 1 - field, j, rows(other, i), :] for i in range(per + GROUP - 1)]
                        for t in range(GROUP):
                            for i in range(per):
                                term = a[i] * b[i + t]
                                totals[t][i] = term if j == 0 else totals[t][i] + term
                    for t in range(GROUP):
                        lag_at = low + jnp.where(is_odd, GROUP - 1 - t, t)
                        for i in range(per):
                            flat[sign, lag_at, z, rows(row, i), :] = totals[t][i]
            for g in range(low + 1, low + GROUP + 1):
                first, length = extent(g)
                if length == 0:
                    continue
                row = jnp.where(is_odd, first, width - first - length)
                x = row + jnp.where(is_odd, cells + skip - g, g - skip - width)
                slot = slots[HMAX + (g if sign == 0 else -g)]
                copies.append((slot, send(made.at[sign, g - 1], row, out, slot, x, length, sem)))
    return copies


def send(here, row, out, slot, x, length, sem):
    pairs = [
        (
            here.at[z, pl.ds(row, length)],
            out.at[jnp.maximum(slot, 0), pl.ds(x, length), :, pl.ds(z * LANES, LANES)],
        )
        for z in range(here.shape[0])
    ]

    @pl.when(slot >= 0)
    def _():
        for source, target in pairs:
            pltpu.make_async_copy(source, target, sem).start()

    return pairs


def finish(copies, sem):
    for slot, pairs in copies:

        @pl.when(slot >= 0)
        def _(pairs=pairs):
            for source, target in pairs:
                pltpu.make_async_copy(source, target, sem).wait()


def local_kernel(offsets_hbm, weights, whole, same, out, wide, slots, offsets, made, zero, load_sem, out_sem):
    load = pltpu.make_async_copy(offsets_hbm, offsets, load_sem)
    load.start()
    tiles, _, used = wide.shape[:3]
    cells, ny = out.shape[1:3]
    odd = lax.axis_index("tile") % 2
    widen(whole.reshape(tiles, 2, used, cells * ny, LANES), wide, PAD + cells, ny, weights)
    widen(same, wide, PAD + (1 - odd) * 2 * cells, ny, weights)
    load.wait()
    for h in range(2 * HMAX + 1):
        slots[h] = -1
    for lag in range(offsets.shape[0]):
        slots[offsets[lag] + HMAX] = lag
    flat = zero.reshape(tiles, cells * ny, LANES)

    def no_lag(i, carry):
        here = pl.ds(pl.multiple_of(i * SUB, SUB), SUB)
        there = pl.ds((PAD + cells) * ny + pl.multiple_of(i * SUB, SUB), SUB)
        for z in range(tiles):
            total = None
            for j in range(used):
                term = wide[z, 0, j, there, :] * wide[z, 1, j, there, :]
                total = term if total is None else total + term
            flat[z, here, :] = total
        return carry

    lax.fori_loop(0, cells * ny // SUB, no_lag, 0)
    copies = [(slots[HMAX], send(zero, 0, out, slots[HMAX], 0, cells, out_sem))]
    copies += image_band(-cells, cells, slots, out, wide, made, out_sem)
    finish(copies, out_sem)


def band_kernel(skip, count, slots, weights, *refs):
    pieces, (out, wide, made, sem) = refs[:count], refs[count + 2 :]
    cells, ny = out.shape[1:3]
    width = pieces[0].shape[3] // ny
    is_odd = lax.axis_index("tile") % 2 == 1
    base = 0
    for piece in pieces:
        widen(piece, wide, PAD + jnp.where(is_odd, 2 * cells + skip, cells - skip - width), ny, weights, base)
        base += piece.shape[2]
    finish(image_band(skip, width, slots, out, wide, made, sem), sem)


def band(skip, slots, weights, pieces, wide, image, share):
    tiles, _, _, n, ny, _ = pieces[0].shape
    count = len(pieces)
    pieces = [in_vmem(p.reshape(tiles, 2, p.shape[2], n * ny, LANES)) for p in pieces]
    return pl.pallas_call(
        functools.partial(band_kernel, skip, count),
        out_shape=(
            jax.ShapeDtypeStruct(image.shape, image.dtype),
            pltpu.VMEM(wide.shape, wide.dtype),
        ),
        in_specs=[SMEM, SMEM] + [VMEM] * (count + 1) + [ANY],
        out_specs=(ANY, VMEM),
        scratch_shapes=[
            pltpu.VMEM((2, HMAX, tiles, n, ny, LANES), jnp.float32),
            pltpu.SemaphoreType.DMA,
        ],
        input_output_aliases={2 + count: 1, 3 + count: 0},
        compiler_params=pltpu.CompilerParams(vmem_limit_bytes=20 << 20),
        cost_estimate=pl.CostEstimate(
            flops=int(8 * share * image.size), bytes_accessed=int(4 * share * image.size), transcendentals=0
        ),
    )(in_smem(slots), in_smem(weights), *pieces, in_vmem(wide), image)


def local_part(offsets, weights, whole, same, shape):
    tiles, _, used, cells, ny, _ = whole.shape
    size = shape[0] * shape[1] * shape[2] * shape[3]
    return pl.pallas_call(
        local_kernel,
        out_shape=(
            jax.ShapeDtypeStruct(shape, jnp.float32),
            pltpu.VMEM((tiles, 2, used, (3 * cells + 2 * PAD) * ny, LANES), jnp.float32),
            pltpu.SMEM((2 * HMAX + 1,), offsets.dtype),
        ),
        in_specs=[ANY, SMEM, VMEM, VMEM],
        out_specs=(ANY, VMEM, SMEM),
        scratch_shapes=[
            pltpu.SMEM(offsets.shape, offsets.dtype),
            pltpu.VMEM((2, HMAX, tiles, cells, ny, LANES), jnp.float32),
            pltpu.VMEM((tiles, cells, ny, LANES), jnp.float32),
            pltpu.SemaphoreType.DMA,
            pltpu.SemaphoreType.DMA,
        ],
        compiler_params=pltpu.CompilerParams(vmem_limit_bytes=20 << 20),
        cost_estimate=pl.CostEstimate(flops=4 * size, bytes_accessed=2 * size, transcendentals=0),
        name="local",
    )(in_hbm(offsets), in_smem(weights), in_vmem(whole), in_vmem(same.reshape(tiles, 2, used, cells * ny, LANES)))


def local(source, receiver, offsets, snap_index):
    _, cells, ny, nz = source.shape
    shape = (offsets.shape[0], cells, ny, nz)
    assert cells == HMAX
    devices = lax.axis_size("tile")
    same = [(i, i ^ 1) for i in range(devices) if i ^ 1 < devices]
    cross = [(i, ((i + 1) ^ 1) - 1) for i in range(1, devices)]
    cross = [(i, j) for i, j in cross if j < devices]
    used, reach = snap_index.shape[0], cells - FAR
    take = functools.partial(select, source=source, receiver=receiver)
    ends, order, weights = select_ends(source, receiver, snap_index, reach)
    got_ends = lax.ppermute(ends, "tile", cross)
    others = take("others", order=order, count=used - ENDS, take=reach)
    got_others = lax.ppermute(others, "tile", cross)
    whole = take("whole", order=order, count=used, take=cells)
    got_same = lax.ppermute(whole, "tile", same)
    far = take("far", order=order, count=used, take=FAR)
    got_far = lax.ppermute(far, "tile", cross)
    made, wide, slots = local_part(offsets, weights, whole, got_same, shape)
    made, wide = band(0, slots, weights, (got_ends, got_others), wide, made, 0.42)
    return band(reach, slots, weights, (got_far,), wide, made, 0.08)[0]


def solution(mesh):
    return jax.shard_map(
        local,
        mesh=mesh,
        in_specs=(P("shot", "tile", None, None), P("shot", "tile", None, None), P(), P()),
        out_specs=P("shot", "tile", None, None),
        check_vma=False,
    )
```

```python
import functools

import jax
import jax.numpy as jnp
from jax import lax
from jax.experimental import pallas as pl
from jax.experimental.pallas import tpu as pltpu
from jax.sharding import PartitionSpec as P

HMAX = 32
LANES = 128
SUB = 8
BLOCK = 4
FAR = 12
ENDS = 2
PAD = 8
GROUP = 4

ANY = pl.BlockSpec(memory_space=pl.ANY)
SMEM = pl.BlockSpec(memory_space=pltpu.SMEM)
VMEM = pl.BlockSpec(memory_space=pltpu.VMEM)


def in_vmem(x):
    return pltpu.with_memory_space_constraint(x, pltpu.VMEM)


def in_smem(x):
    return pltpu.with_memory_space_constraint(x, pltpu.SMEM)


def in_hbm(x):
    return pltpu.with_memory_space_constraint(x, pltpu.HBM)


def gather(source, receiver, chosen, start, out, sem):
    copies = []
    for field, stored in enumerate((source, receiver)):
        for k, snapshot in enumerate(chosen):
            for z in range(out.shape[0]):
                copy = pltpu.make_async_copy(
                    stored.at[snapshot, pl.ds(start, out.shape[3]), :, pl.ds(z * LANES, LANES)],
                    out.at[z, field, k],
                    sem.at[field, k, z],
                )
                copy.start()
                copies.append(copy)
    return copies


def near_start(cells, take):
    return (lax.axis_index("tile") % 2) * (cells - take)


def select_ends_kernel(snap_hbm, source, receiver, out, order, weights, snap, snap_sem, sem):
    load = pltpu.make_async_copy(snap_hbm, snap, snap_sem)
    load.start()
    final = source.shape[0] - 1
    start = near_start(source.shape[1], out.shape[3])
    copies = gather(source, receiver, (0, final), start, out, sem)
    load.wait()
    used = snap.shape[0]
    other = jnp.int32(ENDS)
    for j in range(used):
        snapshot = snap[j]
        is_end = (snapshot == 0) | (snapshot == final)
        at = jnp.where(is_end, jnp.where(snapshot == 0, 0, 1), jnp.minimum(other, used - 1))
        order[at] = snapshot
        weights[at] = (j + 1.0) / used
        other = other + jnp.where(is_end, 0, 1)
    for copy in copies:
        copy.wait()


def select_others_kernel(order, source, receiver, out, sem):
    chosen = [order[k] for k in range(ENDS, order.shape[0])]
    for copy in gather(source, receiver, chosen, near_start(source.shape[1], out.shape[3]), out, sem):
        copy.wait()


def select_rest_kernel(order, source, receiver, whole, far, whole_sem, far_sem):
    cells, take = source.shape[1], far.shape[3]
    chosen = [order[k] for k in range(order.shape[0])]
    start = cells - take - near_start(cells, take)
    copies = gather(source, receiver, chosen, 0, whole, whole_sem)
    copies += gather(source, receiver, chosen, start, far, far_sem)
    for copy in copies:
        copy.wait()


def select_ends(source, receiver, snap_index, take):
    _, _, ny, nz = source.shape
    tiles = nz // LANES
    return pl.pallas_call(
        select_ends_kernel,
        out_shape=(
            pltpu.VMEM((tiles, 2, ENDS, take, ny, LANES), source.dtype),
            pltpu.SMEM(snap_index.shape, snap_index.dtype),
            pltpu.SMEM(snap_index.shape, jnp.float32),
        ),
        in_specs=[ANY, ANY, ANY],
        out_specs=(VMEM, SMEM, SMEM),
        scratch_shapes=[
            pltpu.SMEM(snap_index.shape, snap_index.dtype),
            pltpu.SemaphoreType.DMA,
            pltpu.SemaphoreType.DMA((2, ENDS, tiles)),
        ],
        compiler_params=pltpu.CompilerParams(vmem_limit_bytes=8 << 20),
        name="select_ends",
    )(in_hbm(snap_index), in_hbm(source), in_hbm(receiver))


def select(kernel, source, receiver, order, parts):
    _, _, ny, nz = source.shape
    tiles = nz // LANES
    return pl.pallas_call(
        kernel,
        out_shape=tuple(
            pltpu.VMEM((tiles, 2, count, take, ny, LANES), source.dtype) for count, take in parts
        ),
        in_specs=[SMEM, ANY, ANY],
        out_specs=tuple(VMEM for _ in parts),
        scratch_shapes=[pltpu.SemaphoreType.DMA((2, count, tiles)) for count, _ in parts],
        compiler_params=pltpu.CompilerParams(vmem_limit_bytes=8 << 20),
    )(in_smem(order), in_hbm(source), in_hbm(receiver))


def widen(piece, wide, start, ny, weights, base=0):
    tiles, _, count, rows = piece.shape[:4]
    for k in range(count):
        weight = weights[base + k]
        for z in range(tiles):
            for i in range(0, rows, 16):
                take = pl.ds(i, 16)
                put = pl.ds(pl.multiple_of(start * ny, 16) + i, 16)
                wide[z, 0, base + k, put, :] = piece[z, 0, k, take, :].astype(jnp.float32) * weight
                wide[z, 1, base + k, put, :] = piece[z, 1, k, take, :].astype(jnp.float32)


def image_band(skip, width, slots, out, wide, made, sem):
    tiles, _, used = wide.shape[:3]
    cells, ny = out.shape[1:3]
    is_odd = lax.axis_index("tile") % 2 == 1
    begin = PAD + jnp.where(is_odd, 2 * cells + skip, cells - skip - width)
    flat = made.reshape(2, HMAX, tiles, width * ny, LANES)
    per = BLOCK * ny // SUB

    def extent(g):
        first = max(0, g - cells - skip)
        return first, max(0, min(g - skip, width) - first)

    def rows(cell, i):
        return pl.ds(pl.multiple_of(cell * ny, SUB) + SUB * i, SUB)

    copies = []
    for sign in range(2):
        field = jnp.where(is_odd, 1 - sign, sign)
        lows = range(max(skip, 0), HMAX, GROUP)
        for low in reversed(lows) if skip >= 0 else lows:
            spans = [extent(g) for g in range(low + 1, low + GROUP + 1)]
            spans = [(first, first + length) for first, length in spans if length > 0]
            from_block = min(first for first, _ in spans) // BLOCK
            to_block = -(-max(last for _, last in spans) // BLOCK)
            for m in range(from_block, to_block):
                row = jnp.where(is_odd, BLOCK * m, width - BLOCK * (m + 1))
                anchor = begin + row
                shift = 2 * (low + 1)
                other = anchor + jnp.where(is_odd, -shift - 2 * (GROUP - 1), shift)
                assert cells + skip + BLOCK * m + cells - shift - 2 * (GROUP - 1) >= -PAD
                for z in range(tiles):
                    totals = [[None] * per for _ in range(GROUP)]
                    for j in range(used):
                        a = [wide[z, field, j, rows(anchor, i), :] for i in range(per)]
                        b = [wide[z, 1 - field, j, rows(other, i), :] for i in range(per + GROUP - 1)]
                        for t in range(GROUP):
                            for i in range(per):
                                term = a[i] * b[i + t]
                                totals[t][i] = term if j == 0 else totals[t][i] + term
                    for t in range(GROUP):
                        lag_at = low + jnp.where(is_odd, GROUP - 1 - t, t)
                        for i in range(per):
                            flat[sign, lag_at, z, rows(row, i), :] = totals[t][i]
            for g in range(low + 1, low + GROUP + 1):
                first, length = extent(g)
                if length == 0:
                    continue
                row = jnp.where(is_odd, first, width - first - length)
                x = row + jnp.where(is_odd, cells + skip - g, g - skip - width)
                slot = slots[HMAX + (g if sign == 0 else -g)]
                copies.append((slot, send(made.at[sign, g - 1], row, out, slot, x, length, sem)))
    return copies


def send(here, row, out, slot, x, length, sem):
    pairs = [
        (
            here.at[z, pl.ds(row, length)],
            out.at[jnp.maximum(slot, 0), pl.ds(x, length), :, pl.ds(z * LANES, LANES)],
        )
        for z in range(here.shape[0])
    ]

    @pl.when(slot >= 0)
    def _():
        for source, target in pairs:
            pltpu.make_async_copy(source, target, sem).start()

    return pairs


def finish(copies, sem):
    for slot, pairs in copies:

        @pl.when(slot >= 0)
        def _(pairs=pairs):
            for source, target in pairs:
                pltpu.make_async_copy(source, target, sem).wait()


def local_kernel(offsets_hbm, weights, whole, same, out, wide, slots, offsets, made, zero, load_sem, out_sem):
    load = pltpu.make_async_copy(offsets_hbm, offsets, load_sem)
    load.start()
    tiles, _, used = wide.shape[:3]
    cells, ny = out.shape[1:3]
    odd = lax.axis_index("tile") % 2
    widen(whole.reshape(tiles, 2, used, cells * ny, LANES), wide, PAD + cells, ny, weights)
    widen(same, wide, PAD + (1 - odd) * 2 * cells, ny, weights)
    load.wait()
    for h in range(2 * HMAX + 1):
        slots[h] = -1
    for lag in range(offsets.shape[0]):
        slots[offsets[lag] + HMAX] = lag
    flat = zero.reshape(tiles, cells * ny, LANES)

    def no_lag(i, carry):
        here = pl.ds(pl.multiple_of(i * SUB, SUB), SUB)
        there = pl.ds((PAD + cells) * ny + pl.multiple_of(i * SUB, SUB), SUB)
        for z in range(tiles):
            total = None
            for j in range(used):
                term = wide[z, 0, j, there, :] * wide[z, 1, j, there, :]
                total = term if total is None else total + term
            flat[z, here, :] = total
        return carry

    lax.fori_loop(0, cells * ny // SUB, no_lag, 0)
    copies = [(slots[HMAX], send(zero, 0, out, slots[HMAX], 0, cells, out_sem))]
    copies += image_band(-cells, cells, slots, out, wide, made, out_sem)
    finish(copies, out_sem)


def band_kernel(skip, count, slots, weights, *refs):
    pieces, (out, wide, made, sem) = refs[:count], refs[count + 2 :]
    cells, ny = out.shape[1:3]
    width = pieces[0].shape[3] // ny
    is_odd = lax.axis_index("tile") % 2 == 1
    base = 0
    for piece in pieces:
        widen(piece, wide, PAD + jnp.where(is_odd, 2 * cells + skip, cells - skip - width), ny, weights, base)
        base += piece.shape[2]
    finish(image_band(skip, width, slots, out, wide, made, sem), sem)


def band(skip, slots, weights, pieces, wide, image, share):
    tiles, _, _, n, ny, _ = pieces[0].shape
    count = len(pieces)
    pieces = [in_vmem(p.reshape(tiles, 2, p.shape[2], n * ny, LANES)) for p in pieces]
    return pl.pallas_call(
        functools.partial(band_kernel, skip, count),
        out_shape=(
            jax.ShapeDtypeStruct(image.shape, image.dtype),
            pltpu.VMEM(wide.shape, wide.dtype),
        ),
        in_specs=[SMEM, SMEM] + [VMEM] * (count + 1) + [ANY],
        out_specs=(ANY, VMEM),
        scratch_shapes=[
            pltpu.VMEM((2, HMAX, tiles, n, ny, LANES), jnp.float32),
            pltpu.SemaphoreType.DMA,
        ],
        input_output_aliases={2 + count: 1, 3 + count: 0},
        compiler_params=pltpu.CompilerParams(vmem_limit_bytes=20 << 20),
        cost_estimate=pl.CostEstimate(
            flops=int(8 * share * image.size), bytes_accessed=int(4 * share * image.size), transcendentals=0
        ),
    )(in_smem(slots), in_smem(weights), *pieces, in_vmem(wide), image)


def local_part(offsets, weights, whole, same, shape):
    tiles, _, used, cells, ny, _ = whole.shape
    size = shape[0] * shape[1] * shape[2] * shape[3]
    return pl.pallas_call(
        local_kernel,
        out_shape=(
            jax.ShapeDtypeStruct(shape, jnp.float32),
            pltpu.VMEM((tiles, 2, used, (3 * cells + 2 * PAD) * ny, LANES), jnp.float32),
            pltpu.SMEM((2 * HMAX + 1,), offsets.dtype),
        ),
        in_specs=[ANY, SMEM, VMEM, VMEM],
        out_specs=(ANY, VMEM, SMEM),
        scratch_shapes=[
            pltpu.SMEM(offsets.shape, offsets.dtype),
            pltpu.VMEM((2, HMAX, tiles, cells, ny, LANES), jnp.float32),
            pltpu.VMEM((tiles, cells, ny, LANES), jnp.float32),
            pltpu.SemaphoreType.DMA,
            pltpu.SemaphoreType.DMA,
        ],
        compiler_params=pltpu.CompilerParams(vmem_limit_bytes=20 << 20),
        cost_estimate=pl.CostEstimate(flops=4 * size, bytes_accessed=2 * size, transcendentals=0),
        name="local",
    )(in_hbm(offsets), in_smem(weights), in_vmem(whole), in_vmem(same.reshape(tiles, 2, used, cells * ny, LANES)))


def local(source, receiver, offsets, snap_index):
    _, cells, ny, nz = source.shape
    shape = (offsets.shape[0], cells, ny, nz)
    assert cells == HMAX
    devices = lax.axis_size("tile")
    same = [(i, i ^ 1) for i in range(devices) if i ^ 1 < devices]
    cross = [(i, ((i + 1) ^ 1) - 1) for i in range(1, devices)]
    cross = [(i, j) for i, j in cross if j < devices]
    used, reach = snap_index.shape[0], cells - FAR
    ends, order, weights = select_ends(source, receiver, snap_index, reach)
    got_ends = lax.ppermute(ends, "tile", cross)
    (others,) = select(select_others_kernel, source, receiver, order, ((used - ENDS, reach),))
    got_others = lax.ppermute(others, "tile", cross)
    whole, far = select(select_rest_kernel, source, receiver, order, ((used, cells), (used, FAR)))
    got_same = lax.ppermute(whole, "tile", same)
    got_far = lax.ppermute(far, "tile", cross)
    made, wide, slots = local_part(offsets, weights, whole, got_same, shape)
    made, wide = band(0, slots, weights, (got_ends, got_others), wide, made, 0.42)
    return band(reach, slots, weights, (got_far,), wide, made, 0.08)[0]


def solution(mesh):
    return jax.shard_map(
        local,
        mesh=mesh,
        in_specs=(P("shot", "tile", None, None), P("shot", "tile", None, None), P(), P()),
        out_specs=P("shot", "tile", None, None),
        check_vma=False,
    )
```
